32 devices in a mesh: img: 8 (over y, x, core), feat: 4 (over z).
Axes of the slice: x: 2, y: 2, z: 4, core: 2. Of those that a mesh axis runs over, the one named last changes fastest.
Arguments:
- coeffs: bfloat16 [16384, 512], P('img', 'feat'), may hold values from -16 to 16
- triples: int32 [3, 16384], P(None, 'feat'), may hold values from 0 to 510, as said below
- sketch: int32 [16384, 128], P('feat'), may hold values from -1 to 1
Outputs:
- basis: float32 [16384, 128], P('img')
- projected: float32 [128, 16384], P('img', 'feat')
The draws below stay inside these ranges and needn't reach their ends.
Inputs may be any that keep to these rules, and one draw needn't show every extreme that they name: `triples`: every column is a triple k1, k2, k1 + k2 with k1 and k2 below 256.
All inputs are finite; a program needn't handle non-finite values.
Results may differ from the reference program's by a relative error of at most 0.0044.
Values may be sent and summed in bfloat16 or wider, within the bound.
A program may use at most 192 MiB of HBM per device.

```python
import math
import jax
import jax.numpy as jnp
from jax import lax

COEFS = 512
RANK = 128
IMAGES = 16384
FEATS = 16384


def draw_coeffs(key, part):
    noise_key = jax.random.fold_in(key, 11)
    scale_key = jax.random.fold_in(key, 12)
    row_draw = jax.random.uniform(scale_key, (IMAGES, 1), jnp.float32)
    ramp = jnp.arange(IMAGES, dtype=jnp.float32)[:, None] / IMAGES
    values = jax.random.normal(noise_key, (IMAGES, COEFS), jnp.float32)
    spread = math.log(10.0)
    row_scale = jnp.exp((spread * row_draw + math.log(3.0) * ramp) / 3.0)
    return jnp.clip(values * row_scale, -16.0, 16.0).astype(jnp.bfloat16)


def draw_triples(key, part):
    first_key = jax.random.fold_in(key, 21)
    second_key = jax.random.fold_in(key, 22)
    first_index = jax.random.randint(first_key, (FEATS,), 0, COEFS // 2, dtype=jnp.int32)
    second_index = jax.random.randint(second_key, (FEATS,), 0, COEFS // 2, dtype=jnp.int32)
    return jnp.stack([first_index, second_index, first_index + second_index]).astype(jnp.int32)


def place_ends(drawn, rng, smallest, high):
    dims = drawn.shape
    place = [jax.random.randint(jax.random.fold_in(rng, axis), (), 0, dims[axis]) for axis in range(len(dims))]
    drawn = drawn.at[tuple(place)].set(smallest)
    longest = dims.index(max(dims))
    place[longest] = (place[longest] + 1) % dims[longest]
    return drawn.at[tuple(place)].set(high)


def setup_inputs(seed: int = 0) -> dict:
    key_of = jax.random.split(jax.random.key(seed), 4)
    return {
        "coeffs": draw_coeffs(jax.random.fold_in(key_of[3], 71), 0),
        "triples": draw_triples(jax.random.fold_in(key_of[3], 71), 0),
        "sketch": place_ends(jax.random.randint(key_of[2], (FEATS, RANK), -1, 2), jax.random.fold_in(key_of[2], 1), -1, 1).astype(jnp.int32),
    }


def features_block(coeffs, triples, first_col, block_width):
    chosen_cols = lax.dynamic_slice_in_dim(triples, first_col, block_width, 1)
    widened = coeffs.astype(jnp.float32)
    product = jnp.take(widened, chosen_cols[0], axis=1) * jnp.take(widened, chosen_cols[1], axis=1)
    product = product * jnp.take(widened, chosen_cols[2], axis=1)
    return product.astype(jnp.bfloat16)

def reference(coeffs, triples, sketch):
    total_rows = coeffs.shape[0]
    total_feats = triples.shape[1]
    block_width = min(4096, total_feats)
    block_count = total_feats // block_width
    sketch_scale = (1.5 / total_feats) ** 0.5

    def sketch_step(carry, block_index):
        first_col = (block_index * block_width).astype(jnp.int32)
        feature_tile = features_block(coeffs, triples, first_col, block_width)
        signs = lax.dynamic_slice_in_dim(sketch, first_col, block_width, 0).astype(jnp.bfloat16)
        return (carry + jnp.dot(feature_tile.astype(jnp.float32), signs.astype(jnp.float32), preferred_element_type=jnp.float32), None)
    summed, unused = lax.scan(sketch_step, jnp.zeros((total_rows, RANK), jnp.float32), jnp.arange(block_count, dtype=jnp.int32))
    sketched = summed * sketch_scale
    gram = jnp.dot(sketched.T, sketched, precision=lax.Precision.HIGHEST) / total_rows
    lower = jnp.linalg.cholesky(gram)
    basis = lax.linalg.triangular_solve(lower, sketched.T, left_side=True, lower=True).T

    def project(block_index):
        first_col = (block_index * block_width).astype(jnp.int32)
        feature_tile = features_block(coeffs, triples, first_col, block_width)
        return jnp.dot(basis.T, feature_tile.astype(jnp.float32), precision=lax.Precision.HIGHEST)
    blocks = lax.map(project, jnp.arange(block_count, dtype=jnp.int32))
    projected = jnp.transpose(blocks, (1, 0, 2)).reshape(RANK, total_feats) / jnp.sqrt(jnp.float32(total_rows))
    return (basis, projected)
```

```python
import jax
import jax.numpy as jnp
from jax import lax
from jax.experimental import pallas as pl
from jax.experimental.pallas import tpu as pltpu
from jax.sharding import PartitionSpec as P

CHUNKS = 4


def features_kernel(half, gathered_ref, sel_ref, signs_ref, tile_ref, sum_ref):
    low = gathered_ref[:, :half]
    first = jnp.dot(low, sel_ref[:half], preferred_element_type=jnp.float32)
    second = jnp.dot(low, sel_ref[half : 2 * half], preferred_element_type=jnp.float32)
    third = jnp.dot(gathered_ref[...], sel_ref[2 * half :], preferred_element_type=jnp.float32)
    tile = (first * second * third).astype(jnp.bfloat16)
    tile_ref[...] = tile
    part = jnp.dot(tile, signs_ref[...], preferred_element_type=jnp.float32)

    @pl.when(pl.program_id(0) == 0)
    def _():
        sum_ref[...] = part

    @pl.when(pl.program_id(0) > 0)
    def _():
        sum_ref[...] += part


def features(gathered, selectors, signs):
    rows, coefs = gathered.shape
    feats = selectors.shape[1]
    rank = signs.shape[1]
    half = coefs // 2
    width = min(512, feats)
    return pl.pallas_call(
        lambda *refs: features_kernel(half, *refs),
        grid=(feats // width,),
        in_specs=[
            pl.BlockSpec((rows, coefs), lambda j: (0, 0)),
            pl.BlockSpec((2 * coefs, width), lambda j: (0, j)),
            pl.BlockSpec((width, rank), lambda j: (j, 0)),
        ],
        out_specs=[
            pl.BlockSpec((rows, width), lambda j: (0, j)),
            pl.BlockSpec((rows, rank), lambda j: (0, 0)),
        ],
        out_shape=[
            jax.ShapeDtypeStruct((rows, feats), jnp.bfloat16),
            jax.ShapeDtypeStruct((rows, rank), jnp.float32),
        ],
        compiler_params=pltpu.CompilerParams(vmem_limit_bytes=32 << 20),
        cost_estimate=pl.CostEstimate(
            flops=2 * rows * feats * (2 * coefs + 2 * rank),
            bytes_accessed=2 * feats * (2 * coefs + rows),
            transcendentals=0,
        ),
    )(gathered, selectors, signs)


def on_device(coeffs, triples, sketch):
    rows_here = coeffs.shape[0]
    feats_here = triples.shape[1]
    rank_cols = sketch.shape[1]
    img_count = lax.axis_size("img")
    total_rows = rows_here * img_count
    total_feats = feats_here * lax.axis_size("feat")
    coef_total = coeffs.shape[1] * lax.axis_size("feat")
    half = coef_total // 2

    def selector(index, depth):
        levels = lax.broadcasted_iota(jnp.int32, (depth, feats_here), 0)
        return (levels == triples[index][None, :]).astype(jnp.bfloat16)

    selectors = jnp.concatenate([selector(0, half), selector(1, half), selector(2, coef_total)], axis=0)
    signs = sketch.astype(jnp.bfloat16)
    step = rows_here // CHUNKS
    tiles = []
    sums = []
    for chunk in range(CHUNKS):
        piece = coeffs[chunk * step : (chunk + 1) * step]
        gathered = lax.all_gather(piece, "feat", axis=1, tiled=True)
        tile, part = features(gathered, selectors, signs)
        tiles.append(tile)
        sums.append(lax.psum(part.astype(jnp.bfloat16), "feat"))
    contract = (((0,), (0,)), ((), ()))
    gram = None
    raw = None
    for tile, value in zip(tiles, sums):
        term = lax.dot_general(value, value, contract, preferred_element_type=jnp.float32)
        gram = term if gram is None else gram + term
    sketch_scale = (1.5 / total_feats) ** 0.5
    gram = lax.psum(gram, "img") * (sketch_scale * sketch_scale / total_rows)
    for tile, value in zip(tiles, sums):
        term = lax.dot_general(value, tile, contract, preferred_element_type=jnp.float32)
        raw = term if raw is None else raw + term
    lower = jnp.linalg.cholesky(gram)
    inverse = lax.linalg.triangular_solve(
        lower, jnp.eye(rank_cols, dtype=jnp.float32), left_side=True, lower=True
    ) * sketch_scale
    exact = lax.Precision.HIGHEST
    solved = jnp.dot(inverse, raw, precision=exact) / jnp.sqrt(jnp.float32(total_rows))
    projected = lax.psum_scatter(
        solved.astype(jnp.bfloat16), "img", scatter_dimension=0, tiled=True
    ).astype(jnp.float32)
    stacked = jnp.concatenate(sums, axis=0).astype(jnp.float32)
    basis = jnp.dot(stacked, inverse.T, precision=exact)
    return (basis, projected)


def solution(mesh):
    in_specs = (P("img", "feat"), P(None, "feat"), P("feat", None))
    out_specs = (P("img", None), P("img", "feat"))
    return jax.shard_map(
        on_device, mesh=mesh, in_specs=in_specs, out_specs=out_specs, check_vma=False
    )
```

```python
import functools

import jax
import jax.numpy as jnp
from jax import lax
from jax.experimental import pallas as pl
from jax.experimental.pallas import tpu as pltpu
from jax.sharding import PartitionSpec as P

CHUNKS = 8
MESH = pl.DeviceIdType.MESH
VMEM = pl.BlockSpec(memory_space=pltpu.VMEM)


def greet(axis, peers):
    barrier = pltpu.get_barrier_semaphore()
    for peer in peers:
        pl.semaphore_signal(barrier, inc=1, device_id={axis: peer}, device_id_type=MESH)
    pl.semaphore_wait(barrier, len(peers))


def gather_kernel(count, width, coeffs_ref, sel_ref, signs_ref, tile_ref, sum_ref, blocks, own_sem, send_sem, recv_sem):
    me = lax.axis_index("feat")
    rows, part = coeffs_ref.shape
    step = rows // CHUNKS
    half = count * part // 2
    tiles = signs_ref.shape[0] // width
    barrier = pltpu.get_barrier_semaphore()

    @pl.when(me > 0)
    def _():
        pl.semaphore_signal(barrier, inc=1, device_id={"feat": me - 1}, device_id_type=MESH)

    @pl.when(me < count - 1)
    def _():
        pl.semaphore_signal(barrier, inc=1, device_id={"feat": me + 1}, device_id_type=MESH)

    own = pltpu.make_async_copy(coeffs_ref, blocks.at[me], own_sem)
    own.start()

    @pl.when((me > 0) & (me < count - 1))
    def _():
        pl.semaphore_wait(barrier, 2)

    @pl.when((me == 0) | (me == count - 1))
    def _():
        pl.semaphore_wait(barrier, 1)

    own.wait()

    def copy(side, hop, chunk, source, target):
        span = blocks.at[source, pl.ds(pl.multiple_of(chunk * step, step), step)]
        return pltpu.make_async_remote_copy(
            src_ref=span,
            dst_ref=span,
            send_sem=send_sem.at[side, hop, chunk],
            recv_sem=recv_sem.at[side, hop, chunk],
            device_id={"feat": target},
            device_id_type=MESH,
        )

    def one_round(turn, carry):
        for hop in range(count):
            chunk = turn - hop
            live = (chunk >= 0) & (chunk < CHUNKS)
            if hop > 0:

                @pl.when(live & (me >= hop))
                def _():
                    copy(0, hop - 1, chunk, me - hop, me - 1).wait_recv()

                @pl.when(live & (me + hop < count))
                def _():
                    copy(1, hop - 1, chunk, me + hop, me + 1).wait_recv()

            if hop < count - 1:

                @pl.when(live & (me >= hop) & (me < count - 1))
                def _():
                    copy(0, hop, chunk, me - hop, me + 1).start()

                @pl.when(live & (me + hop < count) & (me > 0))
                def _():
                    copy(1, hop, chunk, me + hop, me - 1).start()

        @pl.when(turn >= count - 1)
        def _():
            first_row = pl.multiple_of((turn - (count - 1)) * step, step)
            here = pl.ds(first_row, step)
            sum_ref[here, :] = jnp.zeros((step, sum_ref.shape[1]), jnp.float32)
            low = jnp.concatenate([blocks[s, here, :] for s in range(count // 2)], axis=1)
            high = jnp.concatenate([blocks[s, here, :] for s in range(count // 2, count)], axis=1)
            full = jnp.concatenate([low, high], axis=1)

            def one_tile(j, unused):
                cols = pl.ds(pl.multiple_of(j * width, width), width)
                first = jnp.dot(low, sel_ref[:half, cols], preferred_element_type=jnp.float32)
                second = jnp.dot(low, sel_ref[half : 2 * half, cols], preferred_element_type=jnp.float32)
                third = jnp.dot(full, sel_ref[2 * half :, cols], preferred_element_type=jnp.float32)
                tile = (first * second * third).astype(jnp.bfloat16)
                tile_ref[here, cols] = tile
                sum_ref[here, :] += jnp.dot(tile, signs_ref[cols, :], preferred_element_type=jnp.float32)
                return unused

            lax.fori_loop(0, tiles, one_tile, 0)

        return carry

    lax.fori_loop(0, CHUNKS + count - 1, one_round, 0)

    def drain(chunk, carry):
        for hop in range(count - 1):

            @pl.when((me >= hop) & (me < count - 1))
            def _():
                copy(0, hop, chunk, me - hop, me + 1).wait_send()

            @pl.when((me + hop < count) & (me > 0))
            def _():
                copy(1, hop, chunk, me + hop, me - 1).wait_send()

        return carry

    lax.fori_loop(0, CHUNKS, drain, 0)


def gather_features(coeffs, selectors, signs, count):
    rows, part = coeffs.shape
    feats, rank = signs.shape
    hops = max(count - 1, 1)
    return pl.pallas_call(
        functools.partial(gather_kernel, count, min(512, feats)),
        in_specs=[VMEM] * 3,
        out_specs=[VMEM] * 2,
        out_shape=[
            jax.ShapeDtypeStruct((rows, feats), jnp.bfloat16),
            jax.ShapeDtypeStruct((rows, rank), jnp.float32),
        ],
        scratch_shapes=[
            pltpu.VMEM((count, rows, part), jnp.bfloat16),
            pltpu.SemaphoreType.DMA,
            pltpu.SemaphoreType.DMA((2, hops, CHUNKS)),
            pltpu.SemaphoreType.DMA((2, hops, CHUNKS)),
        ],
        compiler_params=pltpu.CompilerParams(
            collective_id=0, has_side_effects=True, vmem_limit_bytes=48 << 20
        ),
    )(coeffs, selectors, signs)


def peers_of(me, count):
    return [lax.rem(me + k, count) for k in range(1, count)]


def sum_gather_kernel(count, part_ref, out_ref, slots, full, send_sem, recv_sem, send_again, recv_again):
    me = lax.axis_index("feat")
    peers = peers_of(me, count)
    greet("feat", peers)
    copies = []
    for k, peer in enumerate(peers):
        copies.append(
            pltpu.make_async_remote_copy(
                src_ref=part_ref.at[peer],
                dst_ref=slots.at[k],
                send_sem=send_sem.at[k],
                recv_sem=recv_sem.at[k],
                device_id={"feat": peer},
                device_id_type=MESH,
            )
        )
        copies[-1].start()
    total = part_ref[me].astype(jnp.float32)
    for k, copy in enumerate(copies):
        copy.wait_recv()
        total = total + slots[k].astype(jnp.float32)
    full[me] = total.astype(full.dtype)
    again = []
    for k, peer in enumerate(peers):
        again.append(
            pltpu.make_async_remote_copy(
                src_ref=full.at[me],
                dst_ref=full.at[me],
                send_sem=send_again.at[k],
                recv_sem=recv_again.at[k],
                device_id={"feat": peer},
                device_id_type=MESH,
            )
        )
        again[-1].start()
    for k in range(count - 1):
        source = lax.rem(me + count - 1 - k, count)
        pltpu.make_async_remote_copy(
            src_ref=full.at[source],
            dst_ref=full.at[source],
            send_sem=send_again.at[k],
            recv_sem=recv_again.at[k],
            device_id={"feat": peers[k]},
            device_id_type=MESH,
        ).wait_recv()
    out_ref[...] = full[...]
    for copy in copies + again:
        copy.wait_send()


def sum_gather(part, count):
    rows, rank = part.shape
    blocks = part.reshape(count, rows // count, rank)
    others = max(count - 1, 1)
    out = pl.pallas_call(
        functools.partial(sum_gather_kernel, count),
        in_specs=[VMEM],
        out_specs=VMEM,
        out_shape=jax.ShapeDtypeStruct(blocks.shape, part.dtype),
        scratch_shapes=[
            pltpu.VMEM((others,) + blocks.shape[1:], part.dtype),
            pltpu.VMEM(blocks.shape, part.dtype),
        ]
        + [pltpu.SemaphoreType.DMA((others,))] * 4,
        compiler_params=pltpu.CompilerParams(collective_id=1, has_side_effects=True),
    )(blocks)
    return out.reshape(rows, rank)


def exchange_kernel(count, scatter, part_ref, out_ref, slots, send_sem, recv_sem):
    me = lax.axis_index("img")
    peers = peers_of(me, count)
    greet("img", peers)
    copies = []
    for k, peer in enumerate(peers):
        copies.append(
            pltpu.make_async_remote_copy(
                src_ref=part_ref.at[peer] if scatter else part_ref,
                dst_ref=slots.at[k],
                send_sem=send_sem.at[k],
                recv_sem=recv_sem.at[k],
                device_id={"img": peer},
                device_id_type=MESH,
            )
        )
        copies[-1].start()
    if scatter:
        out_ref[...] = part_ref[me].astype(jnp.float32)
    else:
        slots[count - 1] = part_ref[...]
    for copy in copies:
        copy.wait_recv()
    if scatter:
        for k in range(count - 1):
            out_ref[...] += slots[k].astype(jnp.float32)
    else:
        total = jnp.zeros(out_ref.shape, jnp.float32)
        for sender in range(count):
            slot = lax.rem(me + 2 * count - sender - 1, count)
            total = total + slots[slot]
        out_ref[...] = total
    for copy in copies:
        copy.wait_send()


def exchange(part, count, scatter, collective_id):
    shape = part.shape[1:] if scatter else part.shape
    others = max(count - 1, 1)
    return pl.pallas_call(
        functools.partial(exchange_kernel, count, scatter),
        in_specs=[VMEM],
        out_specs=VMEM,
        out_shape=jax.ShapeDtypeStruct(shape, jnp.float32),
        scratch_shapes=[
            pltpu.VMEM((others + (0 if scatter else 1),) + shape, part.dtype),
            pltpu.SemaphoreType.DMA((others,)),
            pltpu.SemaphoreType.DMA((others,)),
        ],
        compiler_params=pltpu.CompilerParams(collective_id=collective_id, has_side_effects=True),
    )(part)


def on_device(coeffs, triples, sketch):
    rows_here = coeffs.shape[0]
    feats_here = triples.shape[1]
    rank_cols = sketch.shape[1]
    img_count = lax.axis_size("img")
    feat_count = lax.axis_size("feat")
    total_rows = rows_here * img_count
    total_feats = feats_here * feat_count
    coef_total = coeffs.shape[1] * feat_count
    half = coef_total // 2

    def selector(index, depth):
        levels = lax.broadcasted_iota(jnp.int32, (depth, feats_here), 0)
        return (levels == triples[index][None, :]).astype(jnp.bfloat16)

    selectors = jnp.concatenate([selector(0, half), selector(1, half), selector(2, coef_total)], axis=0)
    signs = sketch.astype(jnp.bfloat16)
    tiles, part = gather_features(coeffs, selectors, signs, feat_count)
    value = sum_gather(part.astype(jnp.bfloat16), feat_count)
    contract = (((0,), (0,)), ((), ()))
    gram = lax.dot_general(value, value, contract, preferred_element_type=jnp.float32)
    sketch_scale = (1.5 / total_feats) ** 0.5
    gram = exchange(gram, img_count, False, 2) * (sketch_scale * sketch_scale / total_rows)
    raw = lax.dot_general(value, tiles, contract, preferred_element_type=jnp.float32)
    lower = jnp.linalg.cholesky(gram)
    inverse = lax.linalg.triangular_solve(
        lower, jnp.eye(rank_cols, dtype=jnp.float32), left_side=True, lower=True
    ) * sketch_scale
    exact = lax.Precision.HIGHEST
    solved = jnp.dot(inverse, raw, precision=exact) / jnp.sqrt(jnp.float32(total_rows))
    outgoing = solved.astype(jnp.bfloat16).reshape(img_count, rank_cols // img_count, feats_here)
    projected = exchange(outgoing, img_count, True, 3)
    basis = jnp.dot(value.astype(jnp.float32), inverse.T, precision=exact)
    return (basis, projected)


def solution(mesh):
    in_specs = (P("img", "feat"), P(None, "feat"), P("feat", None))
    out_specs = (P("img", None), P("img", "feat"))
    return jax.shard_map(
        on_device, mesh=mesh, in_specs=in_specs, out_specs=out_specs, check_vma=False
    )
```

```python
import functools

import jax
import jax.numpy as jnp
from jax import lax
from jax.experimental import pallas as pl
from jax.experimental.pallas import tpu as pltpu
from jax.sharding import PartitionSpec as P

CHUNKS = 8
MESH = pl.DeviceIdType.MESH
VMEM = pl.BlockSpec(memory_space=pltpu.VMEM)


def greet(axis, peers):
    barrier = pltpu.get_barrier_semaphore()
    for peer in peers:
        pl.semaphore_signal(barrier, inc=1, device_id={axis: peer}, device_id_type=MESH)
    pl.semaphore_wait(barrier, len(peers))


def gather_kernel(
    count, width, coeffs_ref, triples_ref, sketch_ref, tile_ref, sum_ref, blocks, sel_ref, signs_ref, own_sem, send_sem, recv_sem
):
    me = lax.axis_index("feat")
    rows, part = coeffs_ref.shape
    step = rows // CHUNKS
    half = count * part // 2
    tiles = sketch_ref.shape[0] // width
    spans = ((0, half), (half, half), (2 * half, 2 * half))

    def build(index):
        start, depth = spans[index]

        def one(j, carry):
            cols = pl.ds(pl.multiple_of(j * width, width), width)
            levels = lax.broadcasted_iota(jnp.int32, (depth, width), 0)
            chosen = triples_ref[index : index + 1, cols]
            sel_ref[start : start + depth, cols] = jnp.where(levels == chosen, 1.0, 0.0).astype(jnp.bfloat16)
            if index == 0:
                signs_ref[cols, :] = sketch_ref[cols, :].astype(jnp.float32).astype(jnp.bfloat16)
            return carry

        lax.fori_loop(0, tiles, one, 0)

    barrier = pltpu.get_barrier_semaphore()

    @pl.when(me > 0)
    def _():
        pl.semaphore_signal(barrier, inc=1, device_id={"feat": me - 1}, device_id_type=MESH)

    @pl.when(me < count - 1)
    def _():
        pl.semaphore_signal(barrier, inc=1, device_id={"feat": me + 1}, device_id_type=MESH)

    own = pltpu.make_async_copy(coeffs_ref, blocks.at[me], own_sem)
    own.start()

    @pl.when((me > 0) & (me < count - 1))
    def _():
        pl.semaphore_wait(barrier, 2)

    @pl.when((me == 0) | (me == count - 1))
    def _():
        pl.semaphore_wait(barrier, 1)

    own.wait()

    def copy(side, hop, chunk, source, target):
        span = blocks.at[source, pl.ds(pl.multiple_of(chunk * step, step), step)]
        return pltpu.make_async_remote_copy(
            src_ref=span,
            dst_ref=span,
            send_sem=send_sem.at[side, hop, chunk],
            recv_sem=recv_sem.at[side, hop, chunk],
            device_id={"feat": target},
            device_id_type=MESH,
        )

    def one_round(turn, carry):
        for hop in range(count):
            chunk = turn - hop
            live = (chunk >= 0) & (chunk < CHUNKS)
            if hop > 0:

                @pl.when(live & (me >= hop))
                def _():
                    copy(0, hop - 1, chunk, me - hop, me - 1).wait_recv()

                @pl.when(live & (me + hop < count))
                def _():
                    copy(1, hop - 1, chunk, me + hop, me + 1).wait_recv()

            if hop < count - 1:

                @pl.when(live & (me >= hop) & (me < count - 1))
                def _():
                    copy(0, hop, chunk, me - hop, me + 1).start()

                @pl.when(live & (me + hop < count) & (me > 0))
                def _():
                    copy(1, hop, chunk, me + hop, me - 1).start()

        for index in range(3):

            @pl.when(turn == min(index, count - 2))
            def _():
                build(index)

        @pl.when(turn >= count - 1)
        def _():
            first_row = pl.multiple_of((turn - (count - 1)) * step, step)
            here = pl.ds(first_row, step)
            sum_ref[here, :] = jnp.zeros((step, sum_ref.shape[1]), jnp.float32)
            low = jnp.concatenate([blocks[s, here, :] for s in range(count // 2)], axis=1)
            high = jnp.concatenate([blocks[s, here, :] for s in range(count // 2, count)], axis=1)
            full = jnp.concatenate([low, high], axis=1)

            def one_tile(j, unused):
                cols = pl.ds(pl.multiple_of(j * width, width), width)
                first = jnp.dot(low, sel_ref[:half, cols], preferred_element_type=jnp.float32)
                second = jnp.dot(low, sel_ref[half : 2 * half, cols], preferred_element_type=jnp.float32)
                third = jnp.dot(full, sel_ref[2 * half :, cols], preferred_element_type=jnp.float32)
                tile = (first * second * third).astype(jnp.bfloat16)
                tile_ref[here, cols] = tile
                sum_ref[here, :] += jnp.dot(tile, signs_ref[cols, :], preferred_element_type=jnp.float32)
                return unused

            lax.fori_loop(0, tiles, one_tile, 0, unroll=2)

        return carry

    lax.fori_loop(0, CHUNKS + count - 1, one_round, 0)

    def drain(chunk, carry):
        for hop in range(count - 1):

            @pl.when((me >= hop) & (me < count - 1))
            def _():
                copy(0, hop, chunk, me - hop, me + 1).wait_send()

            @pl.when((me + hop < count) & (me > 0))
            def _():
                copy(1, hop, chunk, me + hop, me - 1).wait_send()

        return carry

    lax.fori_loop(0, CHUNKS, drain, 0)


def gather_features(coeffs, triples, sketch, count):
    rows, part = coeffs.shape
    feats, rank = sketch.shape
    hops = max(count - 1, 1)
    return pl.pallas_call(
        functools.partial(gather_kernel, count, min(512, feats)),
        in_specs=[VMEM] * 3,
        out_specs=[VMEM] * 2,
        out_shape=[
            jax.ShapeDtypeStruct((rows, feats), jnp.bfloat16),
            jax.ShapeDtypeStruct((rows, rank), jnp.float32),
        ],
        scratch_shapes=[
            pltpu.VMEM((count, rows, part), jnp.bfloat16),
            pltpu.VMEM((2 * count * part, feats), jnp.bfloat16),
            pltpu.VMEM((feats, rank), jnp.bfloat16),
            pltpu.SemaphoreType.DMA,
            pltpu.SemaphoreType.DMA((2, hops, CHUNKS)),
            pltpu.SemaphoreType.DMA((2, hops, CHUNKS)),
        ],
        compiler_params=pltpu.CompilerParams(
            collective_id=0, has_side_effects=True, vmem_limit_bytes=24 << 20
        ),
    )(coeffs, triples, sketch)


def peers_of(me, count):
    return [lax.rem(me + k, count) for k in range(1, count)]


def sum_gather_kernel(count, part_ref, out_ref, slots, full, send_sem, recv_sem, send_again, recv_again):
    me = lax.axis_index("feat")
    peers = peers_of(me, count)
    greet("feat", peers)
    copies = []
    for k, peer in enumerate(peers):
        copies.append(
            pltpu.make_async_remote_copy(
                src_ref=part_ref.at[peer],
                dst_ref=slots.at[k],
                send_sem=send_sem.at[k],
                recv_sem=recv_sem.at[k],
                device_id={"feat": peer},
                device_id_type=MESH,
            )
        )
        copies[-1].start()
    total = part_ref[me].astype(jnp.float32)
    for k, copy in enumerate(copies):
        copy.wait_recv()
        total = total + slots[k].astype(jnp.float32)
    full[me] = total.astype(full.dtype)
    again = []
    for k, peer in enumerate(peers):
        again.append(
            pltpu.make_async_remote_copy(
                src_ref=full.at[me],
                dst_ref=full.at[me],
                send_sem=send_again.at[k],
                recv_sem=recv_again.at[k],
                device_id={"feat": peer},
                device_id_type=MESH,
            )
        )
        again[-1].start()
    for k in range(count - 1):
        source = lax.rem(me + count - 1 - k, count)
        pltpu.make_async_remote_copy(
            src_ref=full.at[source],
            dst_ref=full.at[source],
            send_sem=send_again.at[k],
            recv_sem=recv_again.at[k],
            device_id={"feat": peers[k]},
            device_id_type=MESH,
        ).wait_recv()
    out_ref[...] = full[...]
    for copy in copies + again:
        copy.wait_send()


def sum_gather(part, count):
    rows, rank = part.shape
    blocks = part.reshape(count, rows // count, rank)
    others = max(count - 1, 1)
    out = pl.pallas_call(
        functools.partial(sum_gather_kernel, count),
        in_specs=[VMEM],
        out_specs=VMEM,
        out_shape=jax.ShapeDtypeStruct(blocks.shape, part.dtype),
        scratch_shapes=[
            pltpu.VMEM((others,) + blocks.shape[1:], part.dtype),
            pltpu.VMEM(blocks.shape, part.dtype),
        ]
        + [pltpu.SemaphoreType.DMA((others,))] * 4,
        compiler_params=pltpu.CompilerParams(collective_id=1, has_side_effects=True, vmem_limit_bytes=8 << 20),
    )(blocks)
    return out.reshape(rows, rank)


def gram_kernel(count, width, value_ref, tile_ref, gram_ref, raw_ref, turned, slots, send_sem, recv_sem):
    me = lax.axis_index("img")
    peers = peers_of(me, count)
    turned[...] = value_ref[...].T
    slots[count - 1] = jnp.dot(turned[...], value_ref[...], preferred_element_type=jnp.float32)
    greet("img", peers)
    copies = []
    for k, peer in enumerate(peers):
        copies.append(
            pltpu.make_async_remote_copy(
                src_ref=slots.at[count - 1],
                dst_ref=slots.at[k],
                send_sem=send_sem.at[k],
                recv_sem=recv_sem.at[k],
                device_id={"img": peer},
                device_id_type=MESH,
            )
        )
        copies[-1].start()

    def one_tile(j, carry):
        cols = pl.ds(pl.multiple_of(j * width, width), width)
        raw_ref[:, cols] = jnp.dot(turned[...], tile_ref[:, cols], preferred_element_type=jnp.float32)
        return carry

    lax.fori_loop(0, tile_ref.shape[1] // width, one_tile, 0)
    for copy in copies:
        copy.wait_recv()
    total = jnp.zeros(gram_ref.shape, jnp.float32)
    for sender in range(count):
        total = total + slots[lax.rem(me + 2 * count - sender - 1, count)]
    gram_ref[...] = total
    for copy in copies:
        copy.wait_send()


def gram_and_raw(value, tiles, count):
    rows, rank = value.shape
    feats = tiles.shape[1]
    others = max(count - 1, 1)
    return pl.pallas_call(
        functools.partial(gram_kernel, count, min(512, feats)),
        in_specs=[VMEM] * 2,
        out_specs=[VMEM] * 2,
        out_shape=[
            jax.ShapeDtypeStruct((rank, rank), jnp.float32),
            jax.ShapeDtypeStruct((rank, feats), jnp.float32),
        ],
        scratch_shapes=[
            pltpu.VMEM((rank, rows), jnp.bfloat16),
            pltpu.VMEM((others + 1, rank, rank), jnp.float32),
            pltpu.SemaphoreType.DMA((others,)),
            pltpu.SemaphoreType.DMA((others,)),
        ],
        compiler_params=pltpu.CompilerParams(
            collective_id=2, has_side_effects=True, vmem_limit_bytes=16 << 20
        ),
    )(value, tiles)


def rows_kernel(count, part_ref, out_ref, slots, send_sem, recv_sem):
    me = lax.axis_index("img")
    peers = peers_of(me, count)
    greet("img", peers)
    copies = []
    for k, peer in enumerate(peers):
        copies.append(
            pltpu.make_async_remote_copy(
                src_ref=part_ref.at[peer],
                dst_ref=slots.at[k],
                send_sem=send_sem.at[k],
                recv_sem=recv_sem.at[k],
                device_id={"img": peer},
                device_id_type=MESH,
            )
        )
        copies[-1].start()
    out_ref[...] = part_ref[me].astype(jnp.float32)
    for k, copy in enumerate(copies):
        copy.wait_recv()
        out_ref[...] += slots[k].astype(jnp.float32)
    for copy in copies:
        copy.wait_send()


def sum_rows(part, count):
    shape = part.shape[1:]
    others = max(count - 1, 1)
    return pl.pallas_call(
        functools.partial(rows_kernel, count),
        in_specs=[VMEM],
        out_specs=VMEM,
        out_shape=jax.ShapeDtypeStruct(shape, jnp.float32),
        scratch_shapes=[
            pltpu.VMEM((others,) + shape, part.dtype),
            pltpu.SemaphoreType.DMA((others,)),
            pltpu.SemaphoreType.DMA((others,)),
        ],
        compiler_params=pltpu.CompilerParams(collective_id=3, has_side_effects=True, vmem_limit_bytes=12 << 20),
    )(part)


def on_device(coeffs, triples, sketch):
    rows_here = coeffs.shape[0]
    feats_here = triples.shape[1]
    rank_cols = sketch.shape[1]
    img_count = lax.axis_size("img")
    feat_count = lax.axis_size("feat")
    total_rows = rows_here * img_count
    total_feats = feats_here * feat_count
    tiles, part = gather_features(coeffs, triples, sketch, feat_count)
    value = sum_gather(part.astype(jnp.bfloat16), feat_count)
    sketch_scale = (1.5 / total_feats) ** 0.5
    gram, raw = gram_and_raw(value, tiles, img_count)
    gram = gram * (sketch_scale * sketch_scale / total_rows)
    lower = jnp.linalg.cholesky(gram)
    inverse = lax.linalg.triangular_solve(
        lower, jnp.eye(rank_cols, dtype=jnp.float32), left_side=True, lower=True
    ) * sketch_scale
    exact = lax.Precision.HIGHEST
    solved = jnp.dot(inverse, raw, precision=exact) / jnp.sqrt(jnp.float32(total_rows))
    outgoing = solved.astype(jnp.bfloat16).reshape(img_count, rank_cols // img_count, feats_here)
    projected = sum_rows(outgoing, img_count)
    basis = jnp.dot(value.astype(jnp.float32), inverse.T, precision=exact)
    return (basis, projected)


def solution(mesh):
    in_specs = (P("img", "feat"), P(None, "feat"), P("feat", None))
    out_specs = (P("img", None), P("img", "feat"))
    return jax.shard_map(
        on_device, mesh=mesh, in_specs=in_specs, out_specs=out_specs, check_vma=False
    )
```

```python
import functools

import jax
import jax.numpy as jnp
from jax import lax
from jax.experimental import pallas as pl
from jax.experimental.pallas import tpu as pltpu
from jax.sharding import PartitionSpec as P

CHUNKS = 8
MESH = pl.DeviceIdType.MESH
VMEM = pl.BlockSpec(memory_space=pltpu.VMEM)


def greet(axis, peers):
    barrier = pltpu.get_barrier_semaphore()
    for peer in peers:
        pl.semaphore_signal(barrier, inc=1, device_id={axis: peer}, device_id_type=MESH)
    pl.semaphore_wait(barrier, len(peers))


def gather_kernel(
    count, width, coeffs_ref, triples_ref, sketch_ref, tile_ref, value_ref, blocks, sel_ref, signs_ref,
    sum_ref, part_ref, slots, full_ref, own_sem, send_sem, recv_sem, to_sem, from_sem, out_sem, in_sem
):
    me = lax.axis_index("feat")
    rows, part = coeffs_ref.shape
    step = rows // CHUNKS
    half = count * part // 2
    tiles = sketch_ref.shape[0] // width
    spans = ((0, half), (half, half), (2 * half, 2 * half))

    def build(index):
        start, depth = spans[index]

        def one(j, carry):
            cols = pl.ds(pl.multiple_of(j * width, width), width)
            levels = lax.broadcasted_iota(jnp.int32, (depth, width), 0)
            chosen = triples_ref[index : index + 1, cols]
            sel_ref[start : start + depth, cols] = jnp.where(levels == chosen, 1.0, 0.0).astype(jnp.bfloat16)
            if index == 0:
                signs_ref[cols, :] = sketch_ref[cols, :].astype(jnp.float32).astype(jnp.bfloat16)
            return carry

        lax.fori_loop(0, tiles, one, 0)

    own = pltpu.make_async_copy(coeffs_ref, blocks.at[me], own_sem)
    own.start()
    peers = peers_of(me, count)
    piece = step // count
    greet("feat", peers)
    own.wait()

    def copy(side, hop, chunk, source, target):
        span = blocks.at[source, pl.ds(pl.multiple_of(chunk * step, step), step)]
        return pltpu.make_async_remote_copy(
            src_ref=span,
            dst_ref=span,
            send_sem=send_sem.at[side, hop, chunk],
            recv_sem=recv_sem.at[side, hop, chunk],
            device_id={"feat": target},
            device_id_type=MESH,
        )

    def rows_of(chunk, owner):
        return pl.ds(pl.multiple_of(chunk * step + owner * piece, piece), piece)

    def reduce_copy(k, chunk):
        return pltpu.make_async_remote_copy(
            src_ref=part_ref.at[rows_of(chunk, peers[k])],
            dst_ref=slots.at[k, chunk],
            send_sem=to_sem.at[k, chunk],
            recv_sem=from_sem.at[k, chunk],
            device_id={"feat": peers[k]},
            device_id_type=MESH,
        )

    def spread_copy(k, chunk, owner):
        span = full_ref.at[rows_of(chunk, owner)]
        return pltpu.make_async_remote_copy(
            src_ref=span,
            dst_ref=span,
            send_sem=out_sem.at[k, chunk],
            recv_sem=in_sem.at[k, chunk],
            device_id={"feat": peers[k]},
            device_id_type=MESH,
        )

    def one_round(turn, carry):
        for hop in range(count):
            chunk = turn - hop
            live = (chunk >= 0) & (chunk < CHUNKS)
            if hop > 0:

                @pl.when(live & (me >= hop))
                def _():
                    copy(0, hop - 1, chunk, me - hop, me - 1).wait_recv()

                @pl.when(live & (me + hop < count))
                def _():
                    copy(1, hop - 1, chunk, me + hop, me + 1).wait_recv()

            if hop < count - 1:

                @pl.when(live & (me >= hop) & (me < count - 1))
                def _():
                    copy(0, hop, chunk, me - hop, me + 1).start()

                @pl.when(live & (me + hop < count) & (me > 0))
                def _():
                    copy(1, hop, chunk, me + hop, me - 1).start()

        for index in range(3):

            @pl.when(turn == min(index, count - 2))
            def _():
                build(index)

        base = turn - (count - 1)

        @pl.when((base >= 1) & (base <= CHUNKS))
        def _():
            for k in range(count - 1):
                reduce_copy(k, base - 1).start()

        @pl.when(base >= 2)
        def _():
            for k in range(count - 1):
                spread_copy(k, base - 2, me).start()

        @pl.when((base >= 0) & (base < CHUNKS))
        def _():
            first_row = pl.multiple_of(base * step, step)
            here = pl.ds(first_row, step)
            sum_ref[...] = jnp.zeros(sum_ref.shape, jnp.float32)
            low = jnp.concatenate([blocks[s, here, :] for s in range(count // 2)], axis=1)
            high = jnp.concatenate([blocks[s, here, :] for s in range(count // 2, count)], axis=1)
            full = jnp.concatenate([low, high], axis=1)

            def one_tile(j, unused):
                cols = pl.ds(pl.multiple_of(j * width, width), width)
                first = jnp.dot(low, sel_ref[:half, cols], preferred_element_type=jnp.float32)
                second = jnp.dot(low, sel_ref[half : 2 * half, cols], preferred_element_type=jnp.float32)
                third = jnp.dot(full, sel_ref[2 * half :, cols], preferred_element_type=jnp.float32)
                tile = (first * second * third).astype(jnp.bfloat16)
                tile_ref[here, cols] = tile
                sum_ref[...] += jnp.dot(tile, signs_ref[cols, :], preferred_element_type=jnp.float32)
                return unused

            lax.fori_loop(0, tiles, one_tile, 0, unroll=2)
            part_ref[here, :] = sum_ref[...].astype(jnp.bfloat16)

        @pl.when((base >= 1) & (base <= CHUNKS))
        def _():
            mine = rows_of(base - 1, me)
            total = part_ref[mine, :].astype(jnp.float32)
            for k in range(count - 1):
                reduce_copy(k, base - 1).wait_recv()
                total = total + slots[k, base - 1].astype(jnp.float32)
            full_ref[mine, :] = total.astype(jnp.bfloat16)

        return carry

    lax.fori_loop(0, CHUNKS + count + 1, one_round, 0)

    def drain(chunk, carry):
        for k in range(count - 1):
            spread_copy(k, chunk, lax.rem(me + count - 1 - k, count)).wait_recv()
            spread_copy(k, chunk, me).wait_send()
            reduce_copy(k, chunk).wait_send()
        for hop in range(count - 1):

            @pl.when((me >= hop) & (me < count - 1))
            def _():
                copy(0, hop, chunk, me - hop, me + 1).wait_send()

            @pl.when((me + hop < count) & (me > 0))
            def _():
                copy(1, hop, chunk, me + hop, me - 1).wait_send()

        return carry

    lax.fori_loop(0, CHUNKS, drain, 0)
    value_ref[...] = full_ref[...]


def gather_features(coeffs, triples, sketch, count):
    rows, part = coeffs.shape
    feats, rank = sketch.shape
    hops = max(count - 1, 1)
    step = rows // CHUNKS
    return pl.pallas_call(
        functools.partial(gather_kernel, count, min(512, feats)),
        in_specs=[VMEM] * 3,
        out_specs=[VMEM] * 2,
        out_shape=[
            jax.ShapeDtypeStruct((rows, feats), jnp.bfloat16),
            jax.ShapeDtypeStruct((rows, rank), jnp.bfloat16),
        ],
        scratch_shapes=[
            pltpu.VMEM((count, rows, part), jnp.bfloat16),
            pltpu.VMEM((2 * count * part, feats), jnp.bfloat16),
            pltpu.VMEM((feats, rank), jnp.bfloat16),
            pltpu.VMEM((step, rank), jnp.float32),
            pltpu.VMEM((rows, rank), jnp.bfloat16),
            pltpu.VMEM((hops, CHUNKS, step // count, rank), jnp.bfloat16),
            pltpu.VMEM((rows, rank), jnp.bfloat16),
            pltpu.SemaphoreType.DMA,
            pltpu.SemaphoreType.DMA((2, hops, CHUNKS)),
            pltpu.SemaphoreType.DMA((2, hops, CHUNKS)),
        ]
        + [pltpu.SemaphoreType.DMA((hops, CHUNKS))] * 4,
        compiler_params=pltpu.CompilerParams(
            collective_id=0, has_side_effects=True, vmem_limit_bytes=24 << 20
        ),
    )(coeffs, triples, sketch)


def peers_of(me, count):
    return [lax.rem(me + k, count) for k in range(1, count)]


def gram_kernel(count, width, value_ref, tile_ref, gram_ref, raw_ref, turned, slots, send_sem, recv_sem):
    me = lax.axis_index("img")
    peers = peers_of(me, count)
    turned[...] = value_ref[...].T
    slots[count - 1] = jnp.dot(turned[...], value_ref[...], preferred_element_type=jnp.float32)
    greet("img", peers)
    copies = []
    for k, peer in enumerate(peers):
        copies.append(
            pltpu.make_async_remote_copy(
                src_ref=slots.at[count - 1],
                dst_ref=slots.at[k],
                send_sem=send_sem.at[k],
                recv_sem=recv_sem.at[k],
                device_id={"img": peer},
                device_id_type=MESH,
            )
        )
        copies[-1].start()

    def one_tile(j, carry):
        cols = pl.ds(pl.multiple_of(j * width, width), width)
        raw_ref[:, cols] = jnp.dot(turned[...], tile_ref[:, cols], preferred_element_type=jnp.float32)
        return carry

    lax.fori_loop(0, tile_ref.shape[1] // width, one_tile, 0)
    for copy in copies:
        copy.wait_recv()
    total = jnp.zeros(gram_ref.shape, jnp.float32)
    for sender in range(count):
        total = total + slots[lax.rem(me + 2 * count - sender - 1, count)]
    gram_ref[...] = total
    for copy in copies:
        copy.wait_send()


def gram_and_raw(value, tiles, count):
    rows, rank = value.shape
    feats = tiles.shape[1]
    others = max(count - 1, 1)
    return pl.pallas_call(
        functools.partial(gram_kernel, count, min(512, feats)),
        in_specs=[VMEM] * 2,
        out_specs=[VMEM] * 2,
        out_shape=[
            jax.ShapeDtypeStruct((rank, rank), jnp.float32),
            jax.ShapeDtypeStruct((rank, feats), jnp.float32),
        ],
        scratch_shapes=[
            pltpu.VMEM((rank, rows), jnp.bfloat16),
            pltpu.VMEM((others + 1, rank, rank), jnp.float32),
            pltpu.SemaphoreType.DMA((others,)),
            pltpu.SemaphoreType.DMA((others,)),
        ],
        compiler_params=pltpu.CompilerParams(
            collective_id=2, has_side_effects=True, vmem_limit_bytes=16 << 20
        ),
    )(value, tiles)


def rows_kernel(count, part_ref, out_ref, slots, send_sem, recv_sem):
    me = lax.axis_index("img")
    peers = peers_of(me, count)
    greet("img", peers)
    copies = []
    for k, peer in enumerate(peers):
        copies.append(
            pltpu.make_async_remote_copy(
                src_ref=part_ref.at[peer],
                dst_ref=slots.at[k],
                send_sem=send_sem.at[k],
                recv_sem=recv_sem.at[k],
                device_id={"img": peer},
                device_id_type=MESH,
            )
        )
        copies[-1].start()
    out_ref[...] = part_ref[me].astype(jnp.float32)
    for k, copy in enumerate(copies):
        copy.wait_recv()
        out_ref[...] += slots[k].astype(jnp.float32)
    for copy in copies:
        copy.wait_send()


def sum_rows(part, count):
    shape = part.shape[1:]
    others = max(count - 1, 1)
    return pl.pallas_call(
        functools.partial(rows_kernel, count),
        in_specs=[VMEM],
        out_specs=VMEM,
        out_shape=jax.ShapeDtypeStruct(shape, jnp.float32),
        scratch_shapes=[
            pltpu.VMEM((others,) + shape, part.dtype),
            pltpu.SemaphoreType.DMA((others,)),
            pltpu.SemaphoreType.DMA((others,)),
        ],
        compiler_params=pltpu.CompilerParams(collective_id=3, has_side_effects=True, vmem_limit_bytes=12 << 20),
    )(part)


def on_device(coeffs, triples, sketch):
    rows_here = coeffs.shape[0]
    feats_here = triples.shape[1]
    rank_cols = sketch.shape[1]
    img_count = lax.axis_size("img")
    feat_count = lax.axis_size("feat")
    total_rows = rows_here * img_count
    total_feats = feats_here * feat_count
    tiles, value = gather_features(coeffs, triples, sketch, feat_count)
    sketch_scale = (1.5 / total_feats) ** 0.5
    gram, raw = gram_and_raw(value, tiles, img_count)
    gram = gram * (sketch_scale * sketch_scale / total_rows)
    lower = jnp.linalg.cholesky(gram)
    inverse = lax.linalg.triangular_solve(
        lower, jnp.eye(rank_cols, dtype=jnp.float32), left_side=True, lower=True
    ) * sketch_scale
    exact = lax.Precision.HIGHEST
    solved = jnp.dot(inverse, raw, precision=exact) / jnp.sqrt(jnp.float32(total_rows))
    outgoing = solved.astype(jnp.bfloat16).reshape(img_count, rank_cols // img_count, feats_here)
    projected = sum_rows(outgoing, img_count)
    basis = jnp.dot(value.astype(jnp.float32), inverse.T, precision=exact)
    return (basis, projected)


def solution(mesh):
    in_specs = (P("img", "feat"), P(None, "feat"), P("feat", None))
    out_specs = (P("img", None), P("img", "feat"))
    return jax.shard_map(
        on_device, mesh=mesh, in_specs=in_specs, out_specs=out_specs, check_vma=False
    )
```

```python
import functools

import jax
import jax.numpy as jnp
from jax import lax
from jax.experimental import pallas as pl
from jax.experimental.pallas import tpu as pltpu
from jax.sharding import PartitionSpec as P

CHUNKS = 8
MESH = pl.DeviceIdType.MESH
VMEM = pl.BlockSpec(memory_space=pltpu.VMEM)


def greet(axis, peers):
    barrier = pltpu.get_barrier_semaphore()
    for peer in peers:
        pl.semaphore_signal(barrier, inc=1, device_id={axis: peer}, device_id_type=MESH)
    pl.semaphore_wait(barrier, len(peers))


def gather_kernel(
    count, width, coeffs_ref, triples_ref, sketch_ref, tile_ref, value_ref, blocks, sel_ref, signs_ref,
    sum_ref, part_ref, slots, full_ref, own_sem, send_sem, recv_sem, to_sem, from_sem, out_sem, in_sem
):
    me = lax.axis_index("feat")
    rows, part = coeffs_ref.shape
    step = rows // CHUNKS
    half = count * part // 2
    tiles = sketch_ref.shape[0] // width
    spans = ((0, half), (half, half), (2 * half, 2 * half))

    def build(index):
        start, depth = spans[index]

        def one(j, carry):
            cols = pl.ds(pl.multiple_of(j * width, width), width)
            levels = lax.broadcasted_iota(jnp.int32, (depth, width), 0)
            chosen = triples_ref[index : index + 1, cols]
            sel_ref[start : start + depth, cols] = jnp.where(levels == chosen, 1.0, 0.0).astype(jnp.bfloat16)
            if index == 0:
                signs_ref[cols, :] = sketch_ref[cols, :].astype(jnp.float32).astype(jnp.bfloat16)
            return carry

        lax.fori_loop(0, tiles, one, 0)

    own = pltpu.make_async_copy(coeffs_ref, blocks.at[me], own_sem)
    own.start()
    peers = peers_of(me, count)
    piece = step // count
    greet("feat", peers)
    own.wait()

    def copy(side, hop, chunk, source, target):
        span = blocks.at[source, pl.ds(pl.multiple_of(chunk * step, step), step)]
        return pltpu.make_async_remote_copy(
            src_ref=span,
            dst_ref=span,
            send_sem=send_sem.at[side, hop, chunk],
            recv_sem=recv_sem.at[side, hop, chunk],
            device_id={"feat": target},
            device_id_type=MESH,
        )

    def rows_of(chunk, owner):
        return pl.ds(pl.multiple_of(chunk * step + owner * piece, piece), piece)

    def reduce_copy(k, chunk):
        return pltpu.make_async_remote_copy(
            src_ref=part_ref.at[rows_of(chunk, peers[k])],
            dst_ref=slots.at[k, chunk],
            send_sem=to_sem.at[k, chunk],
            recv_sem=from_sem.at[k, chunk],
            device_id={"feat": peers[k]},
            device_id_type=MESH,
        )

    def spread_copy(k, chunk, owner):
        span = full_ref.at[rows_of(chunk, owner)]
        return pltpu.make_async_remote_copy(
            src_ref=span,
            dst_ref=span,
            send_sem=out_sem.at[k, chunk],
            recv_sem=in_sem.at[k, chunk],
            device_id={"feat": peers[k]},
            device_id_type=MESH,
        )

    def one_round(turn, carry):
        for hop in range(count):
            chunk = turn - hop
            live = (chunk >= 0) & (chunk < CHUNKS)
            if hop > 0:

                @pl.when(live & (me >= hop))
                def _():
                    copy(0, hop - 1, chunk, me - hop, me - 1).wait_recv()

                @pl.when(live & (me + hop < count))
                def _():
                    copy(1, hop - 1, chunk, me + hop, me + 1).wait_recv()

            if hop < count - 1:

                @pl.when(live & (me >= hop) & (me < count - 1))
                def _():
                    copy(0, hop, chunk, me - hop, me + 1).start()

                @pl.when(live & (me + hop < count) & (me > 0))
                def _():
                    copy(1, hop, chunk, me + hop, me - 1).start()

        for index in range(3):

            @pl.when(turn == min(index, count - 2))
            def _():
                build(index)

        base = turn - (count - 1)

        @pl.when((base >= 1) & (base <= CHUNKS))
        def _():
            for k in range(count - 1):
                reduce_copy(k, base - 1).start()

        @pl.when(base >= 2)
        def _():
            for k in range(count - 1):
                spread_copy(k, base - 2, me).start()

        @pl.when((base >= 0) & (base < CHUNKS))
        def _():
            first_row = pl.multiple_of(base * step, step)
            here = pl.ds(first_row, step)
            sum_ref[...] = jnp.zeros(sum_ref.shape, jnp.float32)
            low = jnp.concatenate([blocks[s, here, :] for s in range(count // 2)], axis=1)
            high = jnp.concatenate([blocks[s, here, :] for s in range(count // 2, count)], axis=1)
            full = jnp.concatenate([low, high], axis=1)

            def one_tile(j, unused):
                cols = pl.ds(pl.multiple_of(j * width, width), width)
                first = jnp.dot(low, sel_ref[:half, cols], preferred_element_type=jnp.float32)
                second = jnp.dot(low, sel_ref[half : 2 * half, cols], preferred_element_type=jnp.float32)
                third = jnp.dot(full, sel_ref[2 * half :, cols], preferred_element_type=jnp.float32)
                tile = (first * second * third).astype(jnp.bfloat16)
                tile_ref[here, cols] = tile
                sum_ref[...] += jnp.dot(tile, signs_ref[cols, :], preferred_element_type=jnp.float32)
                return unused

            lax.fori_loop(0, tiles, one_tile, 0, unroll=2)
            part_ref[here, :] = sum_ref[...].astype(jnp.bfloat16)

        @pl.when((base >= 1) & (base <= CHUNKS))
        def _():
            mine = rows_of(base - 1, me)
            total = part_ref[mine, :].astype(jnp.float32)
            for k in range(count - 1):
                reduce_copy(k, base - 1).wait_recv()
                total = total + slots[k, base - 1].astype(jnp.float32)
            full_ref[mine, :] = total.astype(jnp.bfloat16)

        return carry

    lax.fori_loop(0, CHUNKS + count + 1, one_round, 0)

    def drain(chunk, carry):
        for k in range(count - 1):
            spread_copy(k, chunk, lax.rem(me + count - 1 - k, count)).wait_recv()
            spread_copy(k, chunk, me).wait_send()
            reduce_copy(k, chunk).wait_send()
        for hop in range(count - 1):

            @pl.when((me >= hop) & (me < count - 1))
            def _():
                copy(0, hop, chunk, me - hop, me + 1).wait_send()

            @pl.when((me + hop < count) & (me > 0))
            def _():
                copy(1, hop, chunk, me + hop, me - 1).wait_send()

        return carry

    lax.fori_loop(0, CHUNKS, drain, 0)
    value_ref[...] = full_ref[...]


def gather_features(coeffs, triples, sketch, count):
    rows, part = coeffs.shape
    feats, rank = sketch.shape
    hops = max(count - 1, 1)
    step = rows // CHUNKS
    return pl.pallas_call(
        functools.partial(gather_kernel, count, min(512, feats)),
        in_specs=[VMEM] * 3,
        out_specs=[VMEM] * 2,
        out_shape=[
            jax.ShapeDtypeStruct((rows, feats), jnp.bfloat16),
            jax.ShapeDtypeStruct((rows, rank), jnp.bfloat16),
        ],
        scratch_shapes=[
            pltpu.VMEM((count, rows, part), jnp.bfloat16),
            pltpu.VMEM((2 * count * part, feats), jnp.bfloat16),
            pltpu.VMEM((feats, rank), jnp.bfloat16),
            pltpu.VMEM((step, rank), jnp.float32),
            pltpu.VMEM((rows, rank), jnp.bfloat16),
            pltpu.VMEM((hops, CHUNKS, step // count, rank), jnp.bfloat16),
            pltpu.VMEM((rows, rank), jnp.bfloat16),
            pltpu.SemaphoreType.DMA,
            pltpu.SemaphoreType.DMA((2, hops, CHUNKS)),
            pltpu.SemaphoreType.DMA((2, hops, CHUNKS)),
        ]
        + [pltpu.SemaphoreType.DMA((hops, CHUNKS))] * 4,
        compiler_params=pltpu.CompilerParams(
            collective_id=0, has_side_effects=True, vmem_limit_bytes=24 << 20
        ),
    )(coeffs, triples, sketch)


def peers_of(me, count):
    return [lax.rem(me + k, count) for k in range(1, count)]


def gram_kernel(count, width, value_ref, tile_ref, gram_ref, raw_ref, turned, slots, send_sem, recv_sem):
    me = lax.axis_index("img")
    peers = peers_of(me, count)
    turned[...] = value_ref[...].T
    slots[count - 1] = jnp.dot(turned[...], value_ref[...], preferred_element_type=jnp.float32)
    greet("img", peers)
    copies = []
    for k, peer in enumerate(peers):
        copies.append(
            pltpu.make_async_remote_copy(
                src_ref=slots.at[count - 1],
                dst_ref=slots.at[k],
                send_sem=send_sem.at[k],
                recv_sem=recv_sem.at[k],
                device_id={"img": peer},
                device_id_type=MESH,
            )
        )
        copies[-1].start()

    def one_tile(j, carry):
        cols = pl.ds(pl.multiple_of(j * width, width), width)
        raw_ref[:, cols] = jnp.dot(turned[...], tile_ref[:, cols], preferred_element_type=jnp.float32)
        return carry

    lax.fori_loop(0, tile_ref.shape[1] // width, one_tile, 0)
    for copy in copies:
        copy.wait_recv()
    total = jnp.zeros(gram_ref.shape, jnp.float32)
    for sender in range(count):
        total = total + slots[lax.rem(me + 2 * count - sender - 1, count)]
    gram_ref[...] = total
    for copy in copies:
        copy.wait_send()


def gram_and_raw(value, tiles, count):
    rows, rank = value.shape
    feats = tiles.shape[1]
    others = max(count - 1, 1)
    return pl.pallas_call(
        functools.partial(gram_kernel, count, min(512, feats)),
        in_specs=[VMEM] * 2,
        out_specs=[VMEM] * 2,
        out_shape=[
            jax.ShapeDtypeStruct((rank, rank), jnp.float32),
            jax.ShapeDtypeStruct((rank, feats), jnp.float32),
        ],
        scratch_shapes=[
            pltpu.VMEM((rank, rows), jnp.bfloat16),
            pltpu.VMEM((others + 1, rank, rank), jnp.float32),
            pltpu.SemaphoreType.DMA((others,)),
            pltpu.SemaphoreType.DMA((others,)),
        ],
        compiler_params=pltpu.CompilerParams(
            collective_id=2, has_side_effects=True, vmem_limit_bytes=16 << 20
        ),
    )(value, tiles)


def factor_kernel(scale, after, gram_ref, out_ref, left, right):
    size = gram_ref.shape[0]
    rows = lax.broadcasted_iota(jnp.int32, (size, size), 0)
    lanes = lax.broadcasted_iota(jnp.int32, (size, size), 1)
    left[...] = gram_ref[...] * scale
    right[...] = jnp.where(rows == lanes, 1.0, 0.0)

    def eliminate(j, carry):
        block = left[...]
        column = jnp.sum(jnp.where(lanes == j, block, 0.0), axis=1, keepdims=True)
        pivot_row = left[pl.ds(j, 1), :]
        pivot = jnp.sum(jnp.where(lanes[:1] == j, pivot_row, 0.0), axis=1, keepdims=True)
        factor = jnp.where(rows[:, :1] > j, column / pivot, 0.0)
        left[...] = block - factor * pivot_row
        right[...] = right[...] - factor * right[pl.ds(j, 1), :]
        return carry

    lax.fori_loop(0, size, eliminate, 0)
    diagonal = jnp.sum(jnp.where(rows == lanes, left[...], 0.0), axis=1, keepdims=True)
    out_ref[...] = right[...] * (after / jnp.sqrt(diagonal))


def inverse_factor(gram, scale, after):
    return pl.pallas_call(
        functools.partial(factor_kernel, scale, after),
        in_specs=[VMEM],
        out_specs=VMEM,
        out_shape=jax.ShapeDtypeStruct(gram.shape, jnp.float32),
        scratch_shapes=[pltpu.VMEM(gram.shape, jnp.float32)] * 2,
        compiler_params=pltpu.CompilerParams(vmem_limit_bytes=8 << 20),
    )(gram)


def rows_kernel(count, part_ref, out_ref, slots, send_sem, recv_sem):
    me = lax.axis_index("img")
    peers = peers_of(me, count)
    greet("img", peers)
    copies = []
    for k, peer in enumerate(peers):
        copies.append(
            pltpu.make_async_remote_copy(
                src_ref=part_ref.at[peer],
                dst_ref=slots.at[k],
                send_sem=send_sem.at[k],
                recv_sem=recv_sem.at[k],
                device_id={"img": peer},
                device_id_type=MESH,
            )
        )
        copies[-1].start()
    out_ref[...] = part_ref[me].astype(jnp.float32)
    for k, copy in enumerate(copies):
        copy.wait_recv()
        out_ref[...] += slots[k].astype(jnp.float32)
    for copy in copies:
        copy.wait_send()


def sum_rows(part, count):
    shape = part.shape[1:]
    others = max(count - 1, 1)
    return pl.pallas_call(
        functools.partial(rows_kernel, count),
        in_specs=[VMEM],
        out_specs=VMEM,
        out_shape=jax.ShapeDtypeStruct(shape, jnp.float32),
        scratch_shapes=[
            pltpu.VMEM((others,) + shape, part.dtype),
            pltpu.SemaphoreType.DMA((others,)),
            pltpu.SemaphoreType.DMA((others,)),
        ],
        compiler_params=pltpu.CompilerParams(collective_id=3, has_side_effects=True, vmem_limit_bytes=12 << 20),
    )(part)


def on_device(coeffs, triples, sketch):
    rows_here = coeffs.shape[0]
    feats_here = triples.shape[1]
    rank_cols = sketch.shape[1]
    img_count = lax.axis_size("img")
    feat_count = lax.axis_size("feat")
    total_rows = rows_here * img_count
    total_feats = feats_here * feat_count
    tiles, value = gather_features(coeffs, triples, sketch, feat_count)
    sketch_scale = (1.5 / total_feats) ** 0.5
    gram, raw = gram_and_raw(value, tiles, img_count)
    inverse = inverse_factor(gram, sketch_scale * sketch_scale / total_rows, sketch_scale)
    exact = lax.Precision.HIGHEST
    solved = jnp.dot(inverse, raw, precision=exact) / jnp.sqrt(jnp.float32(total_rows))
    outgoing = solved.astype(jnp.bfloat16).reshape(img_count, rank_cols // img_count, feats_here)
    projected = sum_rows(outgoing, img_count)
    basis = jnp.dot(value.astype(jnp.float32), inverse.T, precision=exact)
    return (basis, projected)


def solution(mesh):
    in_specs = (P("img", "feat"), P(None, "feat"), P("feat", None))
    out_specs = (P("img", None), P("img", "feat"))
    return jax.shard_map(
        on_device, mesh=mesh, in_specs=in_specs, out_specs=out_specs, check_vma=False
    )
```

```python
import functools

import jax
import jax.numpy as jnp
from jax import lax
from jax.experimental import pallas as pl
from jax.experimental.pallas import tpu as pltpu
from jax.sharding import PartitionSpec as P

CHUNKS = 8
MESH = pl.DeviceIdType.MESH
VMEM = pl.BlockSpec(memory_space=pltpu.VMEM)


def greet(axis, peers):
    barrier = pltpu.get_barrier_semaphore()
    for peer in peers:
        pl.semaphore_signal(barrier, inc=1, device_id={axis: peer}, device_id_type=MESH)
    pl.semaphore_wait(barrier, len(peers))


def gather_kernel(
    count, width, coeffs_ref, triples_ref, sketch_ref, tile_ref, value_ref, blocks, sel_ref, signs_ref,
    sum_ref, part_ref, slots, full_ref, own_sem, send_sem, recv_sem, to_sem, from_sem, out_sem, in_sem
):
    me = lax.axis_index("feat")
    rows, part = coeffs_ref.shape
    step = rows // CHUNKS
    half = count * part // 2
    tiles = sketch_ref.shape[0] // width
    spans = ((0, half), (half, half), (2 * half, 2 * half))

    def build(index):
        start, depth = spans[index]

        def one(j, carry):
            cols = pl.ds(pl.multiple_of(j * width, width), width)
            levels = lax.broadcasted_iota(jnp.int32, (depth, width), 0)
            chosen = triples_ref[index : index + 1, cols]
            sel_ref[start : start + depth, cols] = jnp.where(levels == chosen, 1.0, 0.0).astype(jnp.bfloat16)
            if index == 0:
                signs_ref[cols, :] = sketch_ref[cols, :].astype(jnp.float32).astype(jnp.bfloat16)
            return carry

        lax.fori_loop(0, tiles, one, 0)

    own = pltpu.make_async_copy(coeffs_ref, blocks.at[me], own_sem)
    own.start()
    peers = peers_of(me, count)
    piece = step // count
    greet("feat", peers)
    own.wait()

    def copy(side, hop, chunk, source, target):
        span = blocks.at[source, pl.ds(pl.multiple_of(chunk * step, step), step)]
        return pltpu.make_async_remote_copy(
            src_ref=span,
            dst_ref=span,
            send_sem=send_sem.at[side, hop, chunk],
            recv_sem=recv_sem.at[side, hop, chunk],
            device_id={"feat": target},
            device_id_type=MESH,
        )

    def rows_of(chunk, owner):
        return pl.ds(pl.multiple_of(chunk * step + owner * piece, piece), piece)

    def reduce_copy(k, chunk):
        return pltpu.make_async_remote_copy(
            src_ref=part_ref.at[rows_of(chunk, peers[k])],
            dst_ref=slots.at[k, chunk],
            send_sem=to_sem.at[k, chunk],
            recv_sem=from_sem.at[k, chunk],
            device_id={"feat": peers[k]},
            device_id_type=MESH,
        )

    def spread_copy(k, chunk, owner):
        span = full_ref.at[rows_of(chunk, owner)]
        return pltpu.make_async_remote_copy(
            src_ref=span,
            dst_ref=span,
            send_sem=out_sem.at[k, chunk],
            recv_sem=in_sem.at[k, chunk],
            device_id={"feat": peers[k]},
            device_id_type=MESH,
        )

    def one_round(turn, carry):
        for hop in range(count):
            chunk = turn - hop
            live = (chunk >= 0) & (chunk < CHUNKS)
            if hop > 0:

                @pl.when(live & (me >= hop))
                def _():
                    copy(0, hop - 1, chunk, me - hop, me - 1).wait_recv()

                @pl.when(live & (me + hop < count))
                def _():
                    copy(1, hop - 1, chunk, me + hop, me + 1).wait_recv()

            if hop < count - 1:

                @pl.when(live & (me >= hop) & (me < count - 1))
                def _():
                    copy(0, hop, chunk, me - hop, me + 1).start()

                @pl.when(live & (me + hop < count) & (me > 0))
                def _():
                    copy(1, hop, chunk, me + hop, me - 1).start()

        for index in range(3):

            @pl.when(turn == min(index, count - 2))
            def _():
                build(index)

        base = turn - (count - 1)

        @pl.when((base >= 1) & (base <= CHUNKS))
        def _():
            for k in range(count - 1):
                reduce_copy(k, base - 1).start()

        @pl.when(base >= 2)
        def _():
            for k in range(count - 1):
                spread_copy(k, base - 2, me).start()

        @pl.when((base >= 0) & (base < CHUNKS))
        def _():
            first_row = pl.multiple_of(base * step, step)
            here = pl.ds(first_row, step)
            sum_ref[...] = jnp.zeros(sum_ref.shape, jnp.float32)
            low = jnp.concatenate([blocks[s, here, :] for s in range(count // 2)], axis=1)
            high = jnp.concatenate([blocks[s, here, :] for s in range(count // 2, count)], axis=1)
            full = jnp.concatenate([low, high], axis=1)

            def one_tile(j, unused):
                cols = pl.ds(pl.multiple_of(j * width, width), width)
                first = jnp.dot(low, sel_ref[:half, cols], preferred_element_type=jnp.float32)
                second = jnp.dot(low, sel_ref[half : 2 * half, cols], preferred_element_type=jnp.float32)
                third = jnp.dot(full, sel_ref[2 * half :, cols], preferred_element_type=jnp.float32)
                tile = (first * second * third).astype(jnp.bfloat16)
                tile_ref[here, cols] = tile
                sum_ref[...] += jnp.dot(tile, signs_ref[cols, :], preferred_element_type=jnp.float32)
                return unused

            lax.fori_loop(0, tiles, one_tile, 0, unroll=2)
            part_ref[here, :] = sum_ref[...].astype(jnp.bfloat16)

        @pl.when((base >= 1) & (base <= CHUNKS))
        def _():
            mine = rows_of(base - 1, me)
            total = part_ref[mine, :].astype(jnp.float32)
            for k in range(count - 1):
                reduce_copy(k, base - 1).wait_recv()
                total = total + slots[k, base - 1].astype(jnp.float32)
            full_ref[mine, :] = total.astype(jnp.bfloat16)

        return carry

    lax.fori_loop(0, CHUNKS + count + 1, one_round, 0)

    def drain(chunk, carry):
        for k in range(count - 1):
            spread_copy(k, chunk, lax.rem(me + count - 1 - k, count)).wait_recv()
            spread_copy(k, chunk, me).wait_send()
            reduce_copy(k, chunk).wait_send()
        for hop in range(count - 1):

            @pl.when((me >= hop) & (me < count - 1))
            def _():
                copy(0, hop, chunk, me - hop, me + 1).wait_send()

            @pl.when((me + hop < count) & (me > 0))
            def _():
                copy(1, hop, chunk, me + hop, me - 1).wait_send()

        return carry

    lax.fori_loop(0, CHUNKS, drain, 0)
    value_ref[...] = full_ref[...]


def gather_features(coeffs, triples, sketch, count):
    rows, part = coeffs.shape
    feats, rank = sketch.shape
    hops = max(count - 1, 1)
    step = rows // CHUNKS
    return pl.pallas_call(
        functools.partial(gather_kernel, count, min(512, feats)),
        in_specs=[VMEM] * 3,
        out_specs=[VMEM] * 2,
        out_shape=[
            jax.ShapeDtypeStruct((rows, feats), jnp.bfloat16),
            jax.ShapeDtypeStruct((rows, rank), jnp.bfloat16),
        ],
        scratch_shapes=[
            pltpu.VMEM((count, rows, part), jnp.bfloat16),
            pltpu.VMEM((2 * count * part, feats), jnp.bfloat16),
            pltpu.VMEM((feats, rank), jnp.bfloat16),
            pltpu.VMEM((step, rank), jnp.float32),
            pltpu.VMEM((rows, rank), jnp.bfloat16),
            pltpu.VMEM((hops, CHUNKS, step // count, rank), jnp.bfloat16),
            pltpu.VMEM((rows, rank), jnp.bfloat16),
            pltpu.SemaphoreType.DMA,
            pltpu.SemaphoreType.DMA((2, hops, CHUNKS)),
            pltpu.SemaphoreType.DMA((2, hops, CHUNKS)),
        ]
        + [pltpu.SemaphoreType.DMA((hops, CHUNKS))] * 4,
        compiler_params=pltpu.CompilerParams(
            collective_id=0, has_side_effects=True, vmem_limit_bytes=24 << 20
        ),
    )(coeffs, triples, sketch)


def peers_of(me, count):
    return [lax.rem(me + k, count) for k in range(1, count)]


def gram_kernel(count, width, value_ref, tile_ref, gram_ref, raw_ref, turned, slots, send_sem, recv_sem):
    me = lax.axis_index("img")
    peers = peers_of(me, count)
    turned[...] = value_ref[...].T
    slots[count - 1] = jnp.dot(turned[...], value_ref[...], preferred_element_type=jnp.float32)
    greet("img", peers)
    copies = []
    for k, peer in enumerate(peers):
        copies.append(
            pltpu.make_async_remote_copy(
                src_ref=slots.at[count - 1],
                dst_ref=slots.at[k],
                send_sem=send_sem.at[k],
                recv_sem=recv_sem.at[k],
                device_id={"img": peer},
                device_id_type=MESH,
            )
        )
        copies[-1].start()

    def one_tile(j, carry):
        cols = pl.ds(pl.multiple_of(j * width, width), width)
        raw_ref[:, cols] = jnp.dot(turned[...], tile_ref[:, cols], preferred_element_type=jnp.float32)
        return carry

    lax.fori_loop(0, tile_ref.shape[1] // width, one_tile, 0)
    for copy in copies:
        copy.wait_recv()
    total = jnp.zeros(gram_ref.shape, jnp.float32)
    for sender in range(count):
        total = total + slots[lax.rem(me + 2 * count - sender - 1, count)]
    gram_ref[...] = total
    for copy in copies:
        copy.wait_send()


def gram_and_raw(value, tiles, count):
    rows, rank = value.shape
    feats = tiles.shape[1]
    others = max(count - 1, 1)
    return pl.pallas_call(
        functools.partial(gram_kernel, count, min(512, feats)),
        in_specs=[VMEM] * 2,
        out_specs=[VMEM] * 2,
        out_shape=[
            jax.ShapeDtypeStruct((rank, rank), jnp.float32),
            jax.ShapeDtypeStruct((rank, feats), jnp.float32),
        ],
        scratch_shapes=[
            pltpu.VMEM((rank, rows), jnp.bfloat16),
            pltpu.VMEM((others + 1, rank, rank), jnp.float32),
            pltpu.SemaphoreType.DMA((others,)),
            pltpu.SemaphoreType.DMA((others,)),
        ],
        compiler_params=pltpu.CompilerParams(
            collective_id=2, has_side_effects=True, vmem_limit_bytes=16 << 20
        ),
    )(value, tiles)


def factor_kernel(scale, after, gram_ref, out_ref, left, right):
    size = gram_ref.shape[0]
    rows = lax.broadcasted_iota(jnp.int32, (size, size), 0)
    lanes = lax.broadcasted_iota(jnp.int32, (size, size), 1)
    left[...] = gram_ref[...] * scale
    right[...] = jnp.where(rows == lanes, 1.0, 0.0)

    def eliminate(j, carry):
        block = left[...]
        column = jnp.sum(jnp.where(lanes == j, block, 0.0), axis=1, keepdims=True)
        pivot_row = left[pl.ds(j, 1), :]
        pivot = jnp.sum(jnp.where(lanes[:1] == j, pivot_row, 0.0), axis=1, keepdims=True)
        factor = jnp.where(rows[:, :1] > j, column / pivot, 0.0)
        left[...] = block - factor * pivot_row
        right[...] = right[...] - factor * right[pl.ds(j, 1), :]
        return carry

    lax.fori_loop(0, size, eliminate, 0, unroll=4)
    diagonal = jnp.sum(jnp.where(rows == lanes, left[...], 0.0), axis=1, keepdims=True)
    out_ref[...] = right[...] * (after / jnp.sqrt(diagonal))


def inverse_factor(gram, scale, after):
    return pl.pallas_call(
        functools.partial(factor_kernel, scale, after),
        in_specs=[VMEM],
        out_specs=VMEM,
        out_shape=jax.ShapeDtypeStruct(gram.shape, jnp.float32),
        scratch_shapes=[pltpu.VMEM(gram.shape, jnp.float32)] * 2,
        compiler_params=pltpu.CompilerParams(vmem_limit_bytes=8 << 20),
    )(gram)


def rows_kernel(count, part_ref, out_ref, slots, send_sem, recv_sem):
    me = lax.axis_index("img")
    peers = peers_of(me, count)
    greet("img", peers)
    copies = []
    for k, peer in enumerate(peers):
        copies.append(
            pltpu.make_async_remote_copy(
                src_ref=part_ref.at[peer],
                dst_ref=slots.at[k],
                send_sem=send_sem.at[k],
                recv_sem=recv_sem.at[k],
                device_id={"img": peer},
                device_id_type=MESH,
            )
        )
        copies[-1].start()
    out_ref[...] = part_ref[me].astype(jnp.float32)
    for k, copy in enumerate(copies):
        copy.wait_recv()
        out_ref[...] += slots[k].astype(jnp.float32)
    for copy in copies:
        copy.wait_send()


def sum_rows(part, count):
    shape = part.shape[1:]
    others = max(count - 1, 1)
    return pl.pallas_call(
        functools.partial(rows_kernel, count),
        in_specs=[VMEM],
        out_specs=VMEM,
        out_shape=jax.ShapeDtypeStruct(shape, jnp.float32),
        scratch_shapes=[
            pltpu.VMEM((others,) + shape, part.dtype),
            pltpu.SemaphoreType.DMA((others,)),
            pltpu.SemaphoreType.DMA((others,)),
        ],
        compiler_params=pltpu.CompilerParams(collective_id=3, has_side_effects=True, vmem_limit_bytes=12 << 20),
    )(part)


def on_device(coeffs, triples, sketch):
    rows_here = coeffs.shape[0]
    feats_here = triples.shape[1]
    rank_cols = sketch.shape[1]
    img_count = lax.axis_size("img")
    feat_count = lax.axis_size("feat")
    total_rows = rows_here * img_count
    total_feats = feats_here * feat_count
    tiles, value = gather_features(coeffs, triples, sketch, feat_count)
    sketch_scale = (1.5 / total_feats) ** 0.5
    gram, raw = gram_and_raw(value, tiles, img_count)
    inverse = inverse_factor(gram, sketch_scale * sketch_scale / total_rows, sketch_scale)
    exact = lax.Precision.HIGHEST
    solved = jnp.dot(inverse, raw, precision=exact) / jnp.sqrt(jnp.float32(total_rows))
    outgoing = solved.astype(jnp.bfloat16).reshape(img_count, rank_cols // img_count, feats_here)
    projected = sum_rows(outgoing, img_count)
    basis = jnp.dot(value.astype(jnp.float32), inverse.T, precision=exact)
    return (basis, projected)


def solution(mesh):
    in_specs = (P("img", "feat"), P(None, "feat"), P("feat", None))
    out_specs = (P("img", None), P("img", "feat"))
    return jax.shard_map(
        on_device, mesh=mesh, in_specs=in_specs, out_specs=out_specs, check_vma=False
    )
```
